32 devices in a mesh: cfg: 2 (over x), sx: 16 (over z, y, core).
Axes of the slice: x: 2, y: 2, z: 4, core: 2. Of those that a mesh axis runs over, the one named last changes fastest.
Arguments:
- eigvecs: bfloat16 [512, 2, 3, 16, 1024], P('cfg', None, None, 'sx'), parts along dimension 0, may hold values from -6 to 6
- link_seed: int32 [6], P('cfg'), parts along dimension 0, may hold values from 1 to 46336
- ownership: int32 [2080], replicated, may hold values from 0 to 2079, each once
Outputs:
- elementals: float32 [4160, 96], P(('cfg', 'sx')), parts along dimension 0
The draws below stay inside these ranges and needn't reach their ends.
There are 2 independent parts, one for each index of `cfg`. The reference program is written for one: setup_inputs(seed, part) draws one part's arguments, and reference() takes and returns one part's arrays. A program takes and returns all parts, laid end to end along the dimension named above; an argument that names none is the same for every part. Nothing has to cross between parts.
Inputs may be any that keep to these rules, and one draw needn't show every extreme that they name: ownership is a permutation of the pair tiles 0 to 2079.
All inputs are finite; a program needn't handle non-finite values.
Results may differ from the reference program's by a relative error of at most 0.0029.
Values may be sent and summed in bfloat16 or wider, within the bound.
A program may use at most 192 MiB of HBM per device.

```python
import math
import jax
import jax.numpy as jnp
import numpy as np
from jax import lax

NEV = 256
TM = 4
NY = 16
NZ = 64
PLANE = 1024
NX = 16
PAIRS = 2080


def steps_of(stream_key, extent, pieces, low, high):
    gain = 1.0
    for axis_at, shards_of in pieces:
        steps = jax.random.uniform(jax.random.fold_in(jax.random.fold_in(stream_key, 6), axis_at), (shards_of,), jnp.float32, low / len(pieces), high / len(pieces))
        gain = gain * jnp.repeat(jnp.exp(steps), extent[axis_at] // shards_of).reshape((-1,) + (1,) * (len(extent) - 1 - axis_at))
    return gain


def scatter_about(rng, shape, scale, most, shards=(), kind=jnp.bfloat16):
    drawn = jax.random.normal(rng, shape, jnp.float32) * scale
    if len(shards) > 0:
        drawn = steps_of(rng, shape, shards, -0.22, 0.18) * drawn
    return jnp.clip(drawn, min=-most, max=most).astype(kind)


def setup_inputs(seed: int = 0, part: int = 0) -> dict:
    splits = jax.random.split(jax.random.key(seed), 4)
    part_splits = jax.random.split(jax.random.fold_in(splits[3], part), 4)
    return {
        "eigvecs": scatter_about(part_splits[0], (NEV, 2, 3, NX, PLANE), 1.0, 6.0, ((3, 16),)),
        "link_seed": jax.random.randint(part_splits[1], (3,), 1, 46337).astype(jnp.int32),
        "ownership": jax.random.permutation(splits[2], PAIRS).astype(jnp.int32),
    }


def scramble(seed_value, site_code):
    modulus = 46337
    low_part = site_code % modulus
    high_part = site_code // modulus
    mixed_value = (seed_value * seed_value + low_part) % modulus
    mixed_value = (mixed_value * mixed_value + high_part * 977 + 31) % modulus
    angles = []
    for angle_index in range(7):
        scrambled = (mixed_value + 5171 * angle_index + 1) % modulus
        scrambled = (scrambled * scrambled + low_part) % modulus
        scrambled = (scrambled * scrambled + 12345) % modulus
        angles.append(scrambled.astype(jnp.float32) * (2.0 * math.pi / modulus) - math.pi)
    return angles

def link_field(seed_value, site_code):
    angles = scramble(seed_value, site_code)
    cos_alpha, sin_alpha = (jnp.cos(angles[0]), jnp.sin(angles[0]))
    cos_beta, sin_beta = (jnp.cos(angles[1]), jnp.sin(angles[1]))
    cos_gamma, sin_gamma = (jnp.cos(angles[2]), jnp.sin(angles[2]))
    rotation = [[cos_alpha * cos_beta * cos_gamma - sin_alpha * sin_gamma, -cos_alpha * cos_beta * sin_gamma - sin_alpha * cos_gamma, cos_alpha * sin_beta], [sin_alpha * cos_beta * cos_gamma + cos_alpha * sin_gamma, -sin_alpha * cos_beta * sin_gamma + cos_alpha * cos_gamma, sin_alpha * sin_beta], [-sin_beta * cos_gamma, sin_beta * sin_gamma, cos_beta]]
    phase_left = [angles[3], angles[4], -angles[3] - angles[4]]
    phase_right = [angles[5], angles[6], -angles[5] - angles[6]]
    link_real = jnp.stack([jnp.stack([rotation[row_index][column] * jnp.cos(phase_left[row_index] + phase_right[column]) for column in range(3)]) for row_index in range(3)])
    link_imag = jnp.stack([jnp.stack([rotation[row_index][column] * jnp.sin(phase_left[row_index] + phase_right[column]) for column in range(3)]) for row_index in range(3)])
    return (link_real, link_imag)

def hop_vectors(link_real, link_imag, vectors):
    real_part = vectors[:, 0].astype(jnp.float32)
    imag_part = vectors[:, 1].astype(jnp.float32)
    out_real = []
    out_imag = []
    for colour in range(3):
        acc_real = jnp.zeros(real_part[:, 0].shape, jnp.float32)
        acc_imag = jnp.zeros(real_part[:, 0].shape, jnp.float32)
        for source in range(3):
            u_real = link_real[colour, source]
            u_imag = link_imag[colour, source]
            acc_real = acc_real + u_real * real_part[:, source] - u_imag * imag_part[:, source]
            acc_imag = acc_imag + u_real * imag_part[:, source] + u_imag * real_part[:, source]
        out_real.append(acc_real)
        out_imag.append(acc_imag)
    return jnp.stack([jnp.stack(out_real, 1), jnp.stack(out_imag, 1)], 1).astype(jnp.bfloat16)

def shift_plane(vectors, axis_number):
    shape = vectors.shape
    spread = vectors.reshape(shape[:4] + (NY, NZ))
    return jnp.roll(spread, -1, axis_number).reshape(shape)

def conjugate_stack(vectors):
    return jnp.concatenate([vectors, jnp.stack([-vectors[:, 1], vectors[:, 0]], 1)], 0)

def antisymmetric(products):
    real_part = products[:, 0] - jnp.swapaxes(products[:, 0], 1, 2)
    imag_part = products[:, 1] + jnp.swapaxes(products[:, 1], 1, 2)
    return jnp.stack([real_part, imag_part], 1)

def pick_tiles(products, chosen_rows):
    tile_count = NEV // TM
    tiles = products.reshape(3, 2, tile_count, TM, tile_count, TM).transpose(2, 4, 0, 1, 3, 5)
    return jnp.take(tiles.reshape(tile_count * tile_count, 6 * TM * TM), chosen_rows, axis=0)

def reference(eigvecs, link_seed, ownership):
    width = 6 * PLANE
    plane_index = jnp.arange(PLANE, dtype=jnp.int32)

    def layer_step(total, layer_index):
        layer = lax.dynamic_slice_in_dim(eigvecs, layer_index, 1, 3)
        upper_index = ((layer_index + 1) % NX).astype(jnp.int32)
        nearest = lax.dynamic_slice_in_dim(eigvecs, upper_index, 1, 3)
        site_code = (layer_index * PLANE + plane_index)[None, :]
        hop_x = hop_vectors(*link_field(link_seed[0], site_code), nearest)
        hop_y = hop_vectors(*link_field(link_seed[1], site_code), shift_plane(layer, 4))
        hop_z = hop_vectors(*link_field(link_seed[2], site_code), shift_plane(layer, 5))
        lefts = conjugate_stack(layer).reshape(2 * NEV, width).astype(jnp.float32)
        rights = jnp.concatenate([hop_x, hop_y, hop_z], 0).reshape(3 * NEV, width).astype(jnp.float32)
        term = lax.dot_general(lefts, rights, (((1,), (1,)), ((), ())), precision=lax.Precision.HIGHEST, preferred_element_type=jnp.float32)
        return (total + term, None)
    start_total = jnp.zeros((2 * NEV, 3 * NEV), jnp.float32)
    gram_matrix, _ = lax.scan(layer_step, start_total, jnp.arange(NX, dtype=jnp.int32))
    products = gram_matrix.reshape(2, NEV, 3, NEV).transpose(2, 0, 1, 3)
    normalise = 1.0 / math.sqrt(12.0 * NX * PLANE)
    derived = antisymmetric(products) * normalise
    upper_rows, upper_cols = np.triu_indices(NEV // TM)
    pair_rows = jnp.asarray((upper_rows * (NEV // TM) + upper_cols).astype(np.int32))
    chosen_rows = jnp.take(pair_rows, ownership)
    return pick_tiles(derived, chosen_rows)
```

```python
import functools
import math

import jax
import jax.numpy as jnp
from jax import lax
from jax.experimental import pallas as pl
from jax.experimental.pallas import tpu as pltpu
from jax.sharding import PartitionSpec as P

TM = 4
NZ = 64
MODULUS = 46337
LANES = 128
ROWS = 16
MESH = pl.DeviceIdType.MESH
F32 = jnp.float32
BF16 = jnp.bfloat16


def from_behind(block, axis, distance):
    devices = range(lax.axis_size(axis))
    route = [((i - distance) % len(devices), i) for i in devices]
    return lax.ppermute(block, axis, route)


def quotient(value):
    q = jnp.floor(value.astype(F32) * (1.0 / MODULUS)).astype(jnp.int32)
    rest = value - q * MODULUS
    q = jnp.where(rest < 0, q - 1, jnp.where(rest >= MODULUS, q + 1, q))
    return q


def modulo(value):
    return value - quotient(value) * MODULUS


def links(seed, first_site, shape):
    code = (
        first_site
        + lax.broadcasted_iota(jnp.int32, shape, 0) * LANES
        + lax.broadcasted_iota(jnp.int32, shape, 1)
    )
    high = quotient(code)
    low = code - high * MODULUS
    mixed = modulo(seed * seed + low)
    mixed = modulo(mixed * mixed + high * 977 + 31)
    th = []
    for k in range(7):
        g = modulo(mixed + (5171 * k + 1))
        g = modulo(g * g + low)
        g = modulo(g * g + 12345)
        th.append(g.astype(F32) * (2.0 * math.pi / MODULUS) - math.pi)
    ca, sa = jnp.cos(th[0]), jnp.sin(th[0])
    cb, sb = jnp.cos(th[1]), jnp.sin(th[1])
    cg, sg = jnp.cos(th[2]), jnp.sin(th[2])
    rot = [
        [ca * cb * cg - sa * sg, -ca * cb * sg - sa * cg, ca * sb],
        [sa * cb * cg + ca * sg, -sa * cb * sg + ca * cg, sa * sb],
        [-sb * cg, sb * sg, cb],
    ]
    left = [th[3], th[4], -th[3] - th[4]]
    right = [th[5], th[6], -th[5] - th[6]]
    real, imag = [], []
    for r in range(3):
        for c in range(3):
            angle = left[r] + right[c]
            real.append(rot[r][c] * jnp.cos(angle))
            imag.append(rot[r][c] * jnp.sin(angle))
    return real + imag


def fill_hops(u_ref, d, src_ref, h_ref, kind):
    modes, sites = src_ref.shape[1], src_ref.shape[2]
    chunks = sites // LANES
    lane = lax.broadcasted_iota(jnp.int32, (ROWS, LANES), 1)

    def chunk_step(k, carry):
        u = [u_ref[d, e, pl.ds(k, 1), :] for e in range(18)]
        at = pl.ds(pl.multiple_of(k * LANES, LANES), LANES)
        after = pl.ds(pl.multiple_of(lax.rem(k + 1, chunks) * LANES, LANES), LANES)

        def rows_step(g, carry):
            rows = pl.ds(pl.multiple_of(g * ROWS, ROWS), ROWS)
            low_rows = pl.ds(pl.multiple_of(modes + g * ROWS, ROWS), ROWS)
            vec = []
            for q in range(6):
                x = src_ref[q, rows, at].astype(F32)
                if kind == 1:
                    nxt = src_ref[q, rows, after].astype(F32)
                    x = pltpu.roll(jnp.where(lane < NZ, nxt, x), NZ, 1)
                if kind == 2:
                    x = jnp.where(
                        lane % NZ == NZ - 1,
                        pltpu.roll(x, NZ - 1, 1),
                        pltpu.roll(x, LANES - 1, 1),
                    )
                vec.append(x)
            for c in range(3):
                re = im = None
                for s in range(3):
                    ur, ui = u[3 * c + s], u[9 + 3 * c + s]
                    vr, vi = vec[s], vec[3 + s]
                    a = ur * vr - ui * vi
                    b = ur * vi + ui * vr
                    re = a if re is None else re + a
                    im = b if im is None else im + b
                re16, im16 = re.astype(BF16), im.astype(BF16)
                h_ref[c, rows, at] = re16
                h_ref[c, low_rows, at] = im16
                h_ref[3 + c, rows, at] = im16
                h_ref[3 + c, low_rows, at] = -re16
            return carry

        return lax.fori_loop(0, modes // ROWS, rows_step, carry)

    lax.fori_loop(0, chunks, chunk_step, 0)


def pack_products(v_ref, h_ref, w_ref, base):
    modes = v_ref.shape[1]
    half = modes // 2
    total = None
    for q in range(6):
        term = lax.dot_general(
            v_ref[q], h_ref[q], (((1,), (1,)), ((), ())), preferred_element_type=F32
        )
        total = term if total is None else total + term
    re, im = total[:, :modes], total[:, modes:]
    re = re - re.T
    im = im + im.T
    row = lax.broadcasted_iota(jnp.int32, (half, half), 0)
    col = lax.broadcasted_iota(jnp.int32, (half, half), 1)
    re_mix = jnp.where(row < col, re[:half, :half], re[half:, half:])
    w_ref[base] = jnp.where(row == col, im[half:, half:], re_mix)
    w_ref[base + 1] = re[:half, half:]
    w_ref[base + 2] = jnp.where(row <= col, im[:half, :half], im[half:, half:])
    w_ref[base + 3] = im[:half, half:]


def yz_kernel(seed_ref, v_ref, w_ref, ux_ref, u_ref, h_ref):
    sites = v_ref.shape[2]
    shape = (sites // LANES, LANES)
    first = lax.axis_index("sx") * sites
    for d in (1, 2, 0):
        for e, entry in enumerate(links(seed_ref[d], first, shape)):
            if d == 0:
                ux_ref[0, e] = entry
            else:
                u_ref[d - 1, e] = entry
    for d in (0, 1):
        fill_hops(u_ref, d, v_ref, h_ref, d + 1)
        pack_products(v_ref, h_ref, w_ref, 4 * d)


def x_kernel(ux_ref, v_ref, near_ref, w_ref, h_ref):
    fill_hops(ux_ref, 0, near_ref, h_ref, 0)
    pack_products(v_ref, h_ref, w_ref, 0)


def sum_kernel(chips, w_ref, out_ref, got, part, send, came, mine, full, sems):
    me = lax.axis_index("sx")
    cfg = lax.axis_index("cfg")
    core = lax.rem(me, 2)
    chip = me // 2
    other = 1 - core
    partner = (cfg, chip * 2 + other)

    def chip_at(step):
        return lax.rem(chip + step, chips)

    barrier = pltpu.get_barrier_semaphore()
    pl.semaphore_signal(barrier, inc=1, device_id=partner, device_id_type=MESH)
    for step in range(1, chips):
        pl.semaphore_signal(
            barrier, inc=1, device_id=(cfg, chip_at(step) * 2 + core), device_id_type=MESH
        )
    pl.semaphore_wait(barrier, chips)

    halves = pltpu.make_async_remote_copy(
        src_ref=w_ref.at[other],
        dst_ref=got,
        send_sem=sems.at[0, 0],
        recv_sem=sems.at[1, 0],
        device_id=partner,
        device_id_type=MESH,
    )
    halves.start()
    halves.wait()
    part[...] = w_ref[core] + got[...]
    send[...] = part[...].astype(BF16)

    pieces = []
    for step in range(1, chips):
        to = chip_at(step)
        copy = pltpu.make_async_remote_copy(
            src_ref=send.at[to],
            dst_ref=came.at[step],
            send_sem=sems.at[2, step],
            recv_sem=sems.at[3, step],
            device_id=(cfg, to * 2 + core),
            device_id_type=MESH,
        )
        copy.start()
        pieces.append(copy)
    total = part[chip]
    for step in range(1, chips):
        pieces[step - 1].wait_recv()
        total = total + came[step].astype(F32)
    mine[...] = total.astype(BF16)
    full[core, chip] = total.astype(BF16)

    back = []
    for step in range(1, chips):
        copy = pltpu.make_async_remote_copy(
            src_ref=mine,
            dst_ref=full.at[core, chip],
            send_sem=sems.at[4, step],
            recv_sem=sems.at[5, step],
            device_id=(cfg, chip_at(step) * 2 + core),
            device_id_type=MESH,
        )
        copy.start()
        back.append(copy)
    for copy in back:
        copy.wait_recv()
    halves = pltpu.make_async_remote_copy(
        src_ref=full.at[core],
        dst_ref=full.at[core],
        send_sem=sems.at[0, 1],
        recv_sem=sems.at[1, 1],
        device_id=partner,
        device_id_type=MESH,
    )
    halves.start()
    halves.wait()
    for copy in pieces:
        copy.wait_send()
    for copy in back:
        copy.wait_send()
    out_ref[...] = full[...]


def sum_over_sites(w, collective):
    size = lax.axis_size("sx")
    chips = size // 2
    blocks, rows, lanes = w.shape
    piece = blocks * rows // size
    shape = (2, chips, piece, lanes)
    vmem = pl.BlockSpec(memory_space=pltpu.VMEM)
    out = pl.pallas_call(
        functools.partial(sum_kernel, chips),
        out_shape=jax.ShapeDtypeStruct(shape, BF16),
        in_specs=[vmem],
        out_specs=vmem,
        scratch_shapes=[
            pltpu.VMEM(shape[1:], F32),
            pltpu.VMEM(shape[1:], F32),
            pltpu.VMEM(shape[1:], BF16),
            pltpu.VMEM(shape[1:], BF16),
            pltpu.VMEM(shape[2:], BF16),
            pltpu.VMEM(shape, BF16),
            pltpu.SemaphoreType.DMA((6, max(chips, 2))),
        ],
        compiler_params=pltpu.CompilerParams(
            collective_id=collective, has_side_effects=True
        ),
        name="sum_over_sites" + str(collective),
    )(w.reshape(shape))
    return out.reshape(w.shape)


def tiles_kernel(scale, slot_ref, x_ref, yz_ref, out_ref, m_ref):
    half = x_ref.shape[1]
    modes = 2 * half
    tiles = modes // TM
    slots, entries = out_ref.shape
    row = lax.broadcasted_iota(jnp.int32, (half, half), 0)
    col = lax.broadcasted_iota(jnp.int32, (half, half), 1)
    for d in range(3):
        src, base = (x_ref, 0) if d == 0 else (yz_ref, 4 * d - 4)
        re_w = src[base].astype(F32)
        im_w = src[base + 2].astype(F32)
        re_t, im_t = re_w.T, im_w.T
        zero = jnp.zeros_like(re_w)
        re_top = jnp.where(row < col, re_w, jnp.where(row > col, -re_t, zero))
        re_low = jnp.where(row > col, re_w, jnp.where(row < col, -re_t, zero))
        im_top = jnp.where(row <= col, im_w, im_t)
        im_low = jnp.where(row > col, im_w, jnp.where(row < col, im_t, re_w))
        for t, top, low in ((0, re_top, re_low), (1, im_top, im_low)):
            at = (2 * d + t) * modes
            m_ref[:half, at : at + half] = top.astype(BF16)
            m_ref[:half, at + half : at + modes] = src[base + 2 * t + 1]
            m_ref[half:, at : at + half] = zero.astype(BF16)
            m_ref[half:, at + half : at + modes] = low.astype(BF16)
    slot = slot_ref[...]
    mode = lax.broadcasted_iota(jnp.int32, (slots, modes), 1)
    i = mode // TM
    start = i * tiles - (i * (i - 1)) // 2
    in_row = (slot >= start) & (slot < start + tiles - i)
    i_of = jnp.max(jnp.where(in_row, i, 0), axis=1, keepdims=True)
    j_of = slot - (i_of * tiles - (i_of * (i_of - 1)) // 2) + i_of
    in_col = jnp.concatenate([(i == j_of).astype(F32)] * 6, axis=1)
    place_row = lax.broadcasted_iota(jnp.int32, (6 * modes, entries), 0)
    place_col = lax.broadcasted_iota(jnp.int32, (6 * modes, entries), 1)
    target = place_col - (place_row // modes) * (TM * TM) - place_row % TM
    total = jnp.zeros((slots, entries), F32)
    for r in range(TM):
        pick = (mode == i_of * TM + r).astype(F32).astype(BF16)
        rows = jnp.dot(pick, m_ref[...], preferred_element_type=F32)
        place = (target == r * TM).astype(F32).astype(BF16)
        total = total + jnp.dot(
            (rows * in_col).astype(BF16), place, preferred_element_type=F32
        )
    out_ref[...] = total * scale


def per_device(eigvecs, link_seed, ownership):
    modes, _, _, layers, sites = eigvecs.shape
    size = lax.axis_size("sx")
    me = lax.axis_index("sx")
    half = modes // 2
    extent_x = layers * size
    v = eigvecs.transpose(1, 2, 3, 0, 4).reshape(6, modes, sites)
    near = from_behind(v, "sx", -1)
    vmem = pl.BlockSpec(memory_space=pltpu.VMEM)
    link_shape = (1, 18, sites // LANES, LANES)
    w_yz, u_x = pl.pallas_call(
        yz_kernel,
        out_shape=(
            jax.ShapeDtypeStruct((8, half, half), F32),
            jax.ShapeDtypeStruct(link_shape, F32),
        ),
        in_specs=[pl.BlockSpec(memory_space=pltpu.SMEM), vmem],
        out_specs=(vmem, vmem),
        scratch_shapes=[
            pltpu.VMEM((2,) + link_shape[1:], F32),
            pltpu.VMEM((6, 2 * modes, sites), BF16),
        ],
        name="products_yz",
    )(link_seed, v)
    sum_yz = sum_over_sites(w_yz, 0)
    w_x = pl.pallas_call(
        x_kernel,
        out_shape=jax.ShapeDtypeStruct((4, half, half), F32),
        in_specs=[vmem] * 3,
        out_specs=vmem,
        scratch_shapes=[pltpu.VMEM((6, 2 * modes, sites), BF16)],
        name="products_x",
    )(u_x, v, near)
    sum_x = sum_over_sites(w_x, 1)
    slots = ownership.shape[0] // size
    own = lax.dynamic_slice_in_dim(ownership, me * slots, slots).reshape(slots, 1)
    return pl.pallas_call(
        functools.partial(tiles_kernel, 1.0 / math.sqrt(12.0 * extent_x * sites)),
        out_shape=jax.ShapeDtypeStruct((slots, 6 * TM * TM), F32),
        in_specs=[vmem] * 3,
        out_specs=vmem,
        scratch_shapes=[pltpu.VMEM((modes, 6 * modes), BF16)],
        name="own_tiles",
    )(own, sum_x, sum_yz)


def solution(mesh):
    return jax.shard_map(
        per_device,
        mesh=mesh,
        in_specs=(P("cfg", None, None, "sx", None), P("cfg"), P()),
        out_specs=P(("cfg", "sx"), None),
        check_vma=False,
    )
```

```python
import functools
import math

import jax
import jax.numpy as jnp
from jax import lax
from jax.experimental import pallas as pl
from jax.experimental.pallas import tpu as pltpu
from jax.sharding import PartitionSpec as P

TM = 4
NZ = 64
MODULUS = 46337
LANES = 128
ROWS = 16
PARTS = 2
LARGE = 32 * 1024 * 1024
SMALL = 8 * 1024 * 1024
MESH = pl.DeviceIdType.MESH
F32 = jnp.float32
BF16 = jnp.bfloat16


def from_behind(block, axis, distance):
    devices = range(lax.axis_size(axis))
    route = [((i - distance) % len(devices), i) for i in devices]
    return lax.ppermute(block, axis, route)


def quotient(value):
    q = jnp.floor(value.astype(F32) * (1.0 / MODULUS)).astype(jnp.int32)
    rest = value - q * MODULUS
    q = jnp.where(rest < 0, q - 1, jnp.where(rest >= MODULUS, q + 1, q))
    return q


def modulo(value):
    return value - quotient(value) * MODULUS


def links(seed, first_site, shape):
    code = (
        first_site
        + lax.broadcasted_iota(jnp.int32, shape, 0) * LANES
        + lax.broadcasted_iota(jnp.int32, shape, 1)
    )
    high = quotient(code)
    low = code - high * MODULUS
    mixed = modulo(seed * seed + low)
    mixed = modulo(mixed * mixed + high * 977 + 31)
    th = []
    for k in range(7):
        g = modulo(mixed + (5171 * k + 1))
        g = modulo(g * g + low)
        g = modulo(g * g + 12345)
        th.append(g.astype(F32) * (2.0 * math.pi / MODULUS) - math.pi)
    ca, sa = jnp.cos(th[0]), jnp.sin(th[0])
    cb, sb = jnp.cos(th[1]), jnp.sin(th[1])
    cg, sg = jnp.cos(th[2]), jnp.sin(th[2])
    rot = [
        [ca * cb * cg - sa * sg, -ca * cb * sg - sa * cg, ca * sb],
        [sa * cb * cg + ca * sg, -sa * cb * sg + ca * cg, sa * sb],
        [-sb * cg, sb * sg, cb],
    ]
    left = [th[3], th[4], -th[3] - th[4]]
    right = [th[5], th[6], -th[5] - th[6]]
    real, imag = [], []
    for r in range(3):
        for c in range(3):
            angle = left[r] + right[c]
            real.append(rot[r][c] * jnp.cos(angle))
            imag.append(rot[r][c] * jnp.sin(angle))
    return real + imag


def shift_plane(v_refs, sv_ref, kind):
    wide = 2 * LANES
    part, sites = v_refs[0].shape[1], v_refs[0].shape[2]
    row = lax.broadcasted_iota(jnp.int32, (wide, wide), 0)
    col = lax.broadcasted_iota(jnp.int32, (wide, wide), 1)
    if kind == 1:
        source = col + NZ
    else:
        source = jnp.where(col % NZ == NZ - 1, col - (NZ - 1), col + 1)
    move = (row == source).astype(F32).astype(BF16)
    carry_in = (row + wide == source).astype(F32).astype(BF16)[:LANES]
    for j, v_ref in enumerate(v_refs):
        rows = slice(j * part, (j + 1) * part)

        def component(q, carry, v_ref=v_ref, rows=rows):
            for at in range(0, sites, wide):
                x = jnp.dot(v_ref[q, :, at : at + wide], move, preferred_element_type=F32)
                if kind == 1:
                    after = (at + wide) % sites
                    x = x + jnp.dot(
                        v_ref[q, :, after : after + LANES],
                        carry_in,
                        preferred_element_type=F32,
                    )
                sv_ref[q, rows, at : at + wide] = x.astype(BF16)
            return carry

        lax.fori_loop(0, 6, component, 0)


def fill_hops(u_ref, d, src_ref, h_ref):
    modes, sites = src_ref.shape[1], src_ref.shape[2]

    def chunk_step(k, carry):
        u = [
            jnp.broadcast_to(u_ref[d, e, pl.ds(k, 1), :], (8, LANES)) for e in range(18)
        ]
        at = pl.ds(pl.multiple_of(k * LANES, LANES), LANES)

        def rows_step(g, carry):
            rows = pl.ds(pl.multiple_of(g * ROWS, ROWS), ROWS)
            vec = [src_ref[q, rows, at].astype(F32) for q in range(6)]
            parts = []
            for lo in (0, 8):
                v = [x[lo : lo + 8] for x in vec]
                out = []
                for c in range(3):
                    re = im = None
                    for s in range(3):
                        ur, ui = u[3 * c + s], u[9 + 3 * c + s]
                        a = ur * v[s] - ui * v[3 + s]
                        b = ur * v[3 + s] + ui * v[s]
                        re = a if re is None else re + a
                        im = b if im is None else im + b
                    out.append((re, im))
                parts.append(out)
            for c in range(3):
                for t in range(2):
                    both = jnp.concatenate([parts[0][c][t], parts[1][c][t]], 0)
                    h_ref[3 * t + c, rows, at] = both.astype(BF16)
            return carry

        return lax.fori_loop(0, modes // ROWS, rows_step, carry, unroll=2)

    lax.fori_loop(0, sites // LANES, chunk_step, 0)


def negate_imag(v_refs, nv_ref):
    part = v_refs[0].shape[1]
    for j, v_ref in enumerate(v_refs):
        for c in range(3):
            nv_ref[c, j * part : (j + 1) * part] = -v_ref[3 + c]


def gram(v_refs, nv_ref, h_ref):
    total = None
    for q in range(6):
        if q < 3:
            tail = [nv_ref[q]]
        else:
            tail = [r[q - 3] for r in v_refs]
        left = jnp.concatenate([r[q] for r in v_refs] + tail, 0)
        term = lax.dot_general(
            left, h_ref[q], (((1,), (1,)), ((), ())), preferred_element_type=F32
        )
        total = term if total is None else total + term
    return total


def pack_products(total, w_ref, base):
    modes = total.shape[0] // 2
    half = modes // 2
    re, im = total[:modes], total[modes:]
    row = lax.broadcasted_iota(jnp.int32, (half, half), 0)
    col = lax.broadcasted_iota(jnp.int32, (half, half), 1)
    re_top = re[:half, :half] - re[:half, :half].T
    re_low = re[half:, half:] - re[half:, half:].T
    im_top = im[:half, :half] + im[:half, :half].T
    im_low = im[half:, half:] + im[half:, half:].T
    re_mix = jnp.where(row < col, re_top, re_low)
    w_ref[base] = jnp.where(row == col, im_low, re_mix)
    w_ref[base + 1] = re[:half, half:] - re[half:, :half].T
    w_ref[base + 2] = jnp.where(row <= col, im_top, im_low)
    w_ref[base + 3] = im[:half, half:] + im[half:, :half].T


def yz_kernel(seed_ref, *refs):
    v_refs, (w_ref, ux_ref, u_ref, sv_ref, h_ref, nv_ref) = refs[:-6], refs[-6:]
    sites = v_refs[0].shape[2]
    shape = (sites // LANES, LANES)
    first = lax.axis_index("sx") * sites
    for d in (1, 2, 0):
        for e, entry in enumerate(links(seed_ref[d], first, shape)):
            if d == 0:
                ux_ref[0, e] = entry
            else:
                u_ref[d - 1, e] = entry
    negate_imag(v_refs, nv_ref)
    for d in (0, 1):
        shift_plane(v_refs, sv_ref, d + 1)
        fill_hops(u_ref, d, sv_ref, h_ref)
        pack_products(gram(v_refs, nv_ref, h_ref), w_ref, 4 * d)


def x_kernel(parts, ux_ref, *refs):
    v_refs, near_ref, rest = refs[:parts], refs[parts], refs[parts + 1 :]
    done_refs, (out_ref, h_ref, nv_ref) = rest[:-3], rest[-3:]
    negate_imag(v_refs, nv_ref)
    fill_hops(ux_ref, 0, near_ref, h_ref)
    total = gram(v_refs, nv_ref, h_ref)
    if len(done_refs) == 0 and out_ref.ndim == 2:
        out_ref[...] = total
    else:
        pack_products(
            jnp.concatenate([r[...] for r in done_refs] + [total], 1), out_ref, 0
        )


def sum_kernel(chips, w_ref, out_ref, got, send, came, mine, full, sems):
    me = lax.axis_index("sx")
    cfg = lax.axis_index("cfg")
    core = lax.rem(me, 2)
    chip = me // 2
    other = 1 - core
    partner = (cfg, chip * 2 + other)

    def chip_at(step):
        return lax.rem(chip + step, chips)

    barrier = pltpu.get_barrier_semaphore()
    pl.semaphore_signal(barrier, inc=1, device_id=partner, device_id_type=MESH)
    for step in range(1, chips):
        pl.semaphore_signal(
            barrier, inc=1, device_id=(cfg, chip_at(step) * 2 + core), device_id_type=MESH
        )
    pl.semaphore_wait(barrier, chips)

    def copy_to(src, dst, row, step, device):
        return pltpu.make_async_remote_copy(
            src_ref=src,
            dst_ref=dst,
            send_sem=sems.at[row, step],
            recv_sem=sems.at[row + 1, step],
            device_id=device,
            device_id_type=MESH,
        )

    def same_core(step):
        return (cfg, chip_at(step) * 2 + core)

    order = list(range(1, chips)) + [0]
    halves = {}
    for step in order:
        to = chip_at(step)
        halves[step] = copy_to(w_ref.at[other, to], got.at[to], 0, step, partner)
        halves[step].start()
    pieces = {}
    for step in order[:-1]:
        to = chip_at(step)
        halves[step].wait_recv()
        send[to] = (w_ref[core, to] + got[to]).astype(BF16)
        pieces[step] = copy_to(send.at[to], came.at[step], 2, step, same_core(step))
        pieces[step].start()
    halves[0].wait_recv()
    total = w_ref[core, chip] + got[chip]
    for step in order[:-1]:
        pieces[step].wait_recv()
        total = total + came[step].astype(F32)
    mine[...] = total.astype(BF16)
    full[core, chip] = total.astype(BF16)

    back = {}
    for step in order[:-1]:
        back[step] = copy_to(mine, full.at[core, chip], 4, step, same_core(step))
        back[step].start()
    passed = [copy_to(mine, full.at[core, chip], 6, 0, partner)]
    passed[0].start()
    for step in order[:-1]:
        origin = lax.rem(chip + chips - step, chips)
        back[step].wait_recv()
        passed.append(
            copy_to(full.at[core, origin], full.at[core, origin], 6, step, partner)
        )
        passed[-1].start()
    for copy in passed:
        copy.wait()
    for step in order:
        halves[step].wait_send()
    for step in order[:-1]:
        pieces[step].wait_send()
        back[step].wait_send()
    out_ref[...] = full[...]


def sum_over_sites(w, collective):
    size = lax.axis_size("sx")
    chips = size // 2
    blocks, rows, lanes = w.shape
    piece = blocks * rows // size
    shape = (2, chips, piece, lanes)
    vmem = pl.BlockSpec(memory_space=pltpu.VMEM)
    out = pl.pallas_call(
        functools.partial(sum_kernel, chips),
        out_shape=jax.ShapeDtypeStruct(shape, BF16),
        in_specs=[vmem],
        out_specs=vmem,
        scratch_shapes=[
            pltpu.VMEM(shape[1:], F32),
            pltpu.VMEM(shape[1:], BF16),
            pltpu.VMEM(shape[1:], BF16),
            pltpu.VMEM(shape[2:], BF16),
            pltpu.VMEM(shape, BF16),
            pltpu.SemaphoreType.DMA((8, chips)),
        ],
        compiler_params=pltpu.CompilerParams(
            collective_id=collective, has_side_effects=True, vmem_limit_bytes=SMALL
        ),
        name="sum_over_sites" + str(collective),
    )(w.reshape(shape))
    return out.reshape(w.shape)


def tiles_kernel(directions, scale, slot_ref, src_ref, *refs):
    out_ref, m_ref = refs[-2:]
    half = src_ref.shape[1]
    modes = 2 * half
    tiles = modes // TM
    count = len(directions)
    slots, entries = out_ref.shape
    row = lax.broadcasted_iota(jnp.int32, (half, half), 0)
    col = lax.broadcasted_iota(jnp.int32, (half, half), 1)
    for n in range(count):
        base = 4 * n
        re_w = src_ref[base].astype(F32)
        im_w = src_ref[base + 2].astype(F32)
        re_t, im_t = re_w.T, im_w.T
        zero = jnp.zeros_like(re_w)
        re_top = jnp.where(row < col, re_w, jnp.where(row > col, -re_t, zero))
        re_low = jnp.where(row > col, re_w, jnp.where(row < col, -re_t, zero))
        im_top = jnp.where(row <= col, im_w, im_t)
        im_low = jnp.where(row > col, im_w, jnp.where(row < col, im_t, re_w))
        for t, top, low in ((0, re_top, re_low), (1, im_top, im_low)):
            at = (2 * n + t) * modes
            m_ref[:half, at : at + half] = top.astype(BF16)
            m_ref[:half, at + half : at + modes] = src_ref[base + 2 * t + 1]
            m_ref[half:, at : at + half] = zero.astype(BF16)
            m_ref[half:, at + half : at + modes] = low.astype(BF16)
    slot = slot_ref[...]
    mode = lax.broadcasted_iota(jnp.int32, (slots, modes), 1)
    i = mode // TM
    start = i * tiles - (i * (i - 1)) // 2
    in_row = (slot >= start) & (slot < start + tiles - i)
    i_of = jnp.max(jnp.where(in_row, i, 0), axis=1, keepdims=True)
    j_of = slot - (i_of * tiles - (i_of * (i_of - 1)) // 2) + i_of
    in_col = jnp.concatenate([(i == j_of).astype(F32)] * (2 * count), axis=1)
    place_row = lax.broadcasted_iota(jnp.int32, (2 * count * modes, entries), 0)
    place_col = lax.broadcasted_iota(jnp.int32, (2 * count * modes, entries), 1)
    first = 2 * directions[0] * TM * TM
    target = place_col - first - (place_row // modes) * (TM * TM) - place_row % TM
    total = refs[0][...] if len(refs) == 3 else jnp.zeros((slots, entries), F32)
    for r in range(TM):
        pick = (mode == i_of * TM + r).astype(F32).astype(BF16)
        rows = jnp.dot(pick, m_ref[...], preferred_element_type=F32)
        place = (target == r * TM).astype(F32).astype(BF16)
        total = total + jnp.dot(
            (rows * in_col).astype(BF16), place, preferred_element_type=F32
        )
    out_ref[...] = total * scale


def per_device(eigvecs, link_seed, ownership):
    modes, _, _, layers, sites = eigvecs.shape
    size = lax.axis_size("sx")
    me = lax.axis_index("sx")
    half = modes // 2
    part = modes // PARTS
    extent_x = layers * size
    v = [
        eigvecs[j * part : (j + 1) * part].transpose(1, 2, 3, 0, 4).reshape(6, part, sites)
        for j in range(PARTS)
    ]
    near = [from_behind(block, "sx", -1) for block in v]
    slots = ownership.shape[0] // size
    own = lax.dynamic_slice_in_dim(ownership, me * slots, slots).reshape(slots, 1)
    scale = 1.0 / math.sqrt(12.0 * extent_x * sites)
    vmem = pl.BlockSpec(memory_space=pltpu.VMEM)
    link_shape = (1, 18, sites // LANES, LANES)
    plane = (6, modes, sites)
    negated = pltpu.VMEM((3, modes, sites), BF16)
    large = pltpu.CompilerParams(vmem_limit_bytes=LARGE)
    small = pltpu.CompilerParams(vmem_limit_bytes=SMALL)

    def own_tiles(directions, factor, summed, *added):
        wide = 2 * len(directions) * modes
        return pl.pallas_call(
            functools.partial(tiles_kernel, directions, factor),
            out_shape=jax.ShapeDtypeStruct((slots, 6 * TM * TM), F32),
            in_specs=[vmem] * (2 + len(added)),
            out_specs=vmem,
            scratch_shapes=[pltpu.VMEM((modes, wide), BF16)],
            compiler_params=small,
            name="own_tiles" + str(directions[0]),
        )(own, summed, *added)

    w_yz, u_x = pl.pallas_call(
        yz_kernel,
        out_shape=(
            jax.ShapeDtypeStruct((8, half, half), F32),
            jax.ShapeDtypeStruct(link_shape, F32),
        ),
        in_specs=[pl.BlockSpec(memory_space=pltpu.SMEM)] + [vmem] * PARTS,
        out_specs=(vmem, vmem),
        scratch_shapes=[
            pltpu.VMEM((2,) + link_shape[1:], F32),
            pltpu.VMEM(plane, BF16),
            pltpu.VMEM(plane, BF16),
            negated,
        ],
        compiler_params=large,
        name="products_yz",
    )(link_seed, *v)
    yz = own_tiles((1, 2), 1.0, sum_over_sites(w_yz, 0))
    done = []
    for j in range(PARTS):
        last = j == PARTS - 1
        shape = (4, half, half) if last else (2 * modes, part)
        operands = [u_x, *v, near[j]] + (done if last else [])
        done.append(
            pl.pallas_call(
                functools.partial(x_kernel, PARTS),
                out_shape=jax.ShapeDtypeStruct(shape, F32),
                in_specs=[vmem] * len(operands),
                out_specs=vmem,
                scratch_shapes=[pltpu.VMEM((6, part, sites), BF16), negated],
                compiler_params=large,
                name="products_x" + str(j),
            )(*operands)
        )
    return own_tiles((0,), scale, sum_over_sites(done[-1], 1), yz)


def solution(mesh):
    return jax.shard_map(
        per_device,
        mesh=mesh,
        in_specs=(P("cfg", None, None, "sx", None), P("cfg"), P()),
        out_specs=P(("cfg", "sx"), None),
        check_vma=False,
    )
```

```python
import functools
import math

import jax
import jax.numpy as jnp
from jax import lax
from jax.experimental import pallas as pl
from jax.experimental.pallas import tpu as pltpu
from jax.sharding import PartitionSpec as P

TM = 4
NZ = 64
MODULUS = 46337
LANES = 128
ROWS = 16
PARTS = 4
LARGE = 32 * 1024 * 1024
SMALL = 8 * 1024 * 1024
MESH = pl.DeviceIdType.MESH
F32 = jnp.float32
BF16 = jnp.bfloat16


def from_behind(block, axis, distance):
    devices = range(lax.axis_size(axis))
    route = [((i - distance) % len(devices), i) for i in devices]
    return lax.ppermute(block, axis, route)


def quotient(value):
    q = jnp.floor(value.astype(F32) * (1.0 / MODULUS)).astype(jnp.int32)
    rest = value - q * MODULUS
    q = jnp.where(rest < 0, q - 1, jnp.where(rest >= MODULUS, q + 1, q))
    return q


def modulo(value):
    return value - quotient(value) * MODULUS


def links(seed, first_site, shape):
    code = (
        first_site
        + lax.broadcasted_iota(jnp.int32, shape, 0) * LANES
        + lax.broadcasted_iota(jnp.int32, shape, 1)
    )
    high = quotient(code)
    low = code - high * MODULUS
    mixed = modulo(seed * seed + low)
    mixed = modulo(mixed * mixed + high * 977 + 31)
    th = []
    for k in range(7):
        g = modulo(mixed + (5171 * k + 1))
        g = modulo(g * g + low)
        g = modulo(g * g + 12345)
        th.append(g.astype(F32) * (2.0 * math.pi / MODULUS) - math.pi)
    ca, sa = jnp.cos(th[0]), jnp.sin(th[0])
    cb, sb = jnp.cos(th[1]), jnp.sin(th[1])
    cg, sg = jnp.cos(th[2]), jnp.sin(th[2])
    rot = [
        [ca * cb * cg - sa * sg, -ca * cb * sg - sa * cg, ca * sb],
        [sa * cb * cg + ca * sg, -sa * cb * sg + ca * cg, sa * sb],
        [-sb * cg, sb * sg, cb],
    ]
    left = [th[3], th[4], -th[3] - th[4]]
    right = [th[5], th[6], -th[5] - th[6]]
    real, imag = [], []
    for r in range(3):
        for c in range(3):
            angle = left[r] + right[c]
            real.append(rot[r][c] * jnp.cos(angle))
            imag.append(rot[r][c] * jnp.sin(angle))
    return real + imag


def shift_plane(v_refs, sv_ref, kind):
    wide = 2 * LANES
    part, sites = v_refs[0].shape[1], v_refs[0].shape[2]
    row = lax.broadcasted_iota(jnp.int32, (wide, wide), 0)
    col = lax.broadcasted_iota(jnp.int32, (wide, wide), 1)
    if kind == 1:
        source = col + NZ
    else:
        source = jnp.where(col % NZ == NZ - 1, col - (NZ - 1), col + 1)
    move = (row == source).astype(F32).astype(BF16)
    carry_in = (row + wide == source).astype(F32).astype(BF16)[:LANES]
    for j, v_ref in enumerate(v_refs):
        rows = slice(j * part, (j + 1) * part)

        def component(q, carry, v_ref=v_ref, rows=rows):
            for at in range(0, sites, wide):
                x = jnp.dot(v_ref[q, :, at : at + wide], move, preferred_element_type=F32)
                if kind == 1:
                    after = (at + wide) % sites
                    x = x + jnp.dot(
                        v_ref[q, :, after : after + LANES],
                        carry_in,
                        preferred_element_type=F32,
                    )
                sv_ref[q, rows, at : at + wide] = x.astype(BF16)
            return carry

        lax.fori_loop(0, 6, component, 0)


def fill_hops(u_ref, d, src_ref, h_ref):
    modes, sites = src_ref.shape[1], src_ref.shape[2]

    def chunk_step(k, carry):
        u = [
            jnp.broadcast_to(u_ref[d, e, pl.ds(k, 1), :], (8, LANES)) for e in range(18)
        ]
        at = pl.ds(pl.multiple_of(k * LANES, LANES), LANES)

        def rows_step(g, carry):
            rows = pl.ds(pl.multiple_of(g * ROWS, ROWS), ROWS)
            vec = [src_ref[q, rows, at].astype(F32) for q in range(6)]
            parts = []
            for lo in (0, 8):
                v = [x[lo : lo + 8] for x in vec]
                out = []
                for c in range(3):
                    re = im = None
                    for s in range(3):
                        ur, ui = u[3 * c + s], u[9 + 3 * c + s]
                        a = ur * v[s] - ui * v[3 + s]
                        b = ur * v[3 + s] + ui * v[s]
                        re = a if re is None else re + a
                        im = b if im is None else im + b
                    out.append((re, im))
                parts.append(out)
            for c in range(3):
                for t in range(2):
                    both = jnp.concatenate([parts[0][c][t], parts[1][c][t]], 0)
                    h_ref[3 * t + c, rows, at] = both.astype(BF16)
            return carry

        return lax.fori_loop(0, modes // ROWS, rows_step, carry, unroll=2)

    lax.fori_loop(0, sites // LANES, chunk_step, 0)


def negate_imag(v_refs, nv_ref):
    part = v_refs[0].shape[1]
    for j, v_ref in enumerate(v_refs):
        for c in range(3):
            nv_ref[c, j * part : (j + 1) * part] = -v_ref[3 + c]


def gram(v_refs, nv_ref, h_ref):
    total = None
    for q in range(6):
        if q < 3:
            tail = [nv_ref[q]]
        else:
            tail = [r[q - 3] for r in v_refs]
        left = jnp.concatenate([r[q] for r in v_refs] + tail, 0)
        term = lax.dot_general(
            left, h_ref[q], (((1,), (1,)), ((), ())), preferred_element_type=F32
        )
        total = term if total is None else total + term
    return total


def pack_products(total, w_ref, base):
    modes = total.shape[0] // 2
    half = modes // 2
    re, im = total[:modes], total[modes:]
    row = lax.broadcasted_iota(jnp.int32, (half, half), 0)
    col = lax.broadcasted_iota(jnp.int32, (half, half), 1)
    re_top = re[:half, :half] - re[:half, :half].T
    re_low = re[half:, half:] - re[half:, half:].T
    im_top = im[:half, :half] + im[:half, :half].T
    im_low = im[half:, half:] + im[half:, half:].T
    re_mix = jnp.where(row < col, re_top, re_low)
    w_ref[base] = jnp.where(row == col, im_low, re_mix)
    w_ref[base + 1] = re[:half, half:] - re[half:, :half].T
    w_ref[base + 2] = jnp.where(row <= col, im_top, im_low)
    w_ref[base + 3] = im[:half, half:] + im[half:, :half].T


def yz_kernel(seed_ref, *refs):
    v_refs, (w_ref, ux_ref, u_ref, sv_ref, h_ref, nv_ref) = refs[:-6], refs[-6:]
    sites = v_refs[0].shape[2]
    shape = (sites // LANES, LANES)
    first = lax.axis_index("sx") * sites
    for d in (1, 2, 0):
        for e, entry in enumerate(links(seed_ref[d], first, shape)):
            if d == 0:
                ux_ref[0, e] = entry
            else:
                u_ref[d - 1, e] = entry
    negate_imag(v_refs, nv_ref)
    for d in (0, 1):
        shift_plane(v_refs, sv_ref, d + 1)
        fill_hops(u_ref, d, sv_ref, h_ref)
        pack_products(gram(v_refs, nv_ref, h_ref), w_ref, 4 * d)


def x_kernel(parts, ux_ref, *refs):
    v_refs, near_ref, rest = refs[:parts], refs[parts], refs[parts + 1 :]
    done_refs, (out_ref, h_ref, nv_ref) = rest[:-3], rest[-3:]
    negate_imag(v_refs, nv_ref)
    fill_hops(ux_ref, 0, near_ref, h_ref)
    total = gram(v_refs, nv_ref, h_ref)
    if len(done_refs) == 0 and out_ref.ndim == 2:
        out_ref[...] = total
    else:
        pack_products(
            jnp.concatenate([r[...] for r in done_refs] + [total], 1), out_ref, 0
        )


def copy_to(src, dst, sems, row, step, device):
    return pltpu.make_async_remote_copy(
        src_ref=src,
        dst_ref=dst,
        send_sem=sems.at[row, step],
        recv_sem=sems.at[row + 1, step],
        device_id=device,
        device_id_type=MESH,
    )


def core_sum_kernel(w_ref, out_ref, got, sems):
    me = lax.axis_index("sx")
    core = lax.rem(me, 2)
    partner = (lax.axis_index("cfg"), (me // 2) * 2 + 1 - core)
    barrier = pltpu.get_barrier_semaphore()
    pl.semaphore_signal(barrier, inc=1, device_id=partner, device_id_type=MESH)
    pl.semaphore_wait(barrier, 1)
    copy = copy_to(w_ref.at[1 - core], got, sems, 0, 0, partner)
    copy.start()
    copy.wait()
    out_ref[...] = (w_ref[core] + got[...]).astype(BF16)


def sum_kernel(chips, w_ref, yz_ref, x_out, yz_out, got, send, came, mine, full, sems):
    me = lax.axis_index("sx")
    cfg = lax.axis_index("cfg")
    core = lax.rem(me, 2)
    chip = me // 2
    other = 1 - core
    partner = (cfg, chip * 2 + other)
    rows = w_ref.shape[2]

    def chip_at(step):
        return lax.rem(chip + step, chips)

    def same_core(step):
        return (cfg, chip_at(step) * 2 + core)

    barrier = pltpu.get_barrier_semaphore()
    pl.semaphore_signal(barrier, inc=1, device_id=partner, device_id_type=MESH)
    for step in range(1, chips):
        pl.semaphore_signal(
            barrier, inc=1, device_id=same_core(step), device_id_type=MESH
        )
    pl.semaphore_wait(barrier, chips)

    order = list(range(1, chips)) + [0]
    halves, pieces, back = {}, {}, {}
    for step in order:
        to = chip_at(step)
        halves[step] = copy_to(w_ref.at[other, to], got.at[to], sems, 0, step, partner)
        halves[step].start()
    for step in order[:-1]:
        to = chip_at(step)
        send[to, rows:] = yz_ref[to]
        halves[step].wait_recv()
        send[to, :rows] = (w_ref[core, to] + got[to]).astype(BF16)
        pieces[step] = copy_to(
            send.at[to], came.at[step], sems, 2, step, same_core(step)
        )
        pieces[step].start()
    halves[0].wait_recv()
    total = jnp.concatenate(
        [w_ref[core, chip] + got[chip], yz_ref[chip].astype(F32)], 0
    )
    for step in order[:-1]:
        pieces[step].wait_recv()
        total = total + came[step].astype(F32)
    mine[...] = total.astype(BF16)
    full[core, chip] = total.astype(BF16)

    for step in order[:-1]:
        back[step] = copy_to(mine, full.at[core, chip], sems, 4, step, same_core(step))
        back[step].start()
    passed = [copy_to(mine, full.at[core, chip], sems, 6, 0, partner)]
    passed[0].start()
    for step in order[:-1]:
        origin = lax.rem(chip + chips - step, chips)
        block = full.at[core, origin]
        back[step].wait_recv()
        passed.append(copy_to(block, block, sems, 6, step, partner))
        passed[-1].start()
    for copy in passed:
        copy.wait()
    for step in order:
        halves[step].wait_send()
    for step in order[:-1]:
        pieces[step].wait_send()
        back[step].wait_send()
    x_out[...] = full[:, :, :rows]
    yz_out[...] = full[:, :, rows:]


def split_rows(w):
    size = lax.axis_size("sx")
    blocks, rows, lanes = w.shape
    return w.reshape(2, size // 2, blocks * rows // size, lanes)


def sum_over_cores(w):
    parts = split_rows(w)
    vmem = pl.BlockSpec(memory_space=pltpu.VMEM)
    return pl.pallas_call(
        core_sum_kernel,
        out_shape=jax.ShapeDtypeStruct(parts.shape[1:], BF16),
        in_specs=[vmem],
        out_specs=vmem,
        scratch_shapes=[
            pltpu.VMEM(parts.shape[1:], F32),
            pltpu.SemaphoreType.DMA((2, 1)),
        ],
        compiler_params=pltpu.CompilerParams(
            collective_id=0, has_side_effects=True, vmem_limit_bytes=SMALL
        ),
        name="sum_over_cores",
    )(parts)


def sum_over_sites(w, part_yz):
    parts = split_rows(w)
    _, chips, rows, lanes = parts.shape
    rows_yz = part_yz.shape[1]
    both = (chips, rows + rows_yz, lanes)
    vmem = pl.BlockSpec(memory_space=pltpu.VMEM)
    x, yz = pl.pallas_call(
        functools.partial(sum_kernel, chips),
        out_shape=(
            jax.ShapeDtypeStruct((2, chips, rows, lanes), BF16),
            jax.ShapeDtypeStruct((2, chips, rows_yz, lanes), BF16),
        ),
        in_specs=[vmem] * 2,
        out_specs=(vmem, vmem),
        scratch_shapes=[
            pltpu.VMEM((chips, rows, lanes), F32),
            pltpu.VMEM(both, BF16),
            pltpu.VMEM(both, BF16),
            pltpu.VMEM(both[1:], BF16),
            pltpu.VMEM((2,) + both, BF16),
            pltpu.SemaphoreType.DMA((8, chips)),
        ],
        compiler_params=pltpu.CompilerParams(
            collective_id=1, has_side_effects=True, vmem_limit_bytes=SMALL
        ),
        name="sum_over_sites",
    )(parts, part_yz)
    return x.reshape(w.shape), yz.reshape(-1, *w.shape[1:])


def tiles_kernel(scale, slot_ref, x_ref, yz_ref, out_ref, m_ref):
    half = x_ref.shape[1]
    modes = 2 * half
    tiles = modes // TM
    count = 3
    slots, entries = out_ref.shape
    row = lax.broadcasted_iota(jnp.int32, (half, half), 0)
    col = lax.broadcasted_iota(jnp.int32, (half, half), 1)
    for n in range(count):
        src_ref, base = (x_ref, 0) if n == 0 else (yz_ref, 4 * n - 4)
        re_w = src_ref[base].astype(F32)
        im_w = src_ref[base + 2].astype(F32)
        re_t, im_t = re_w.T, im_w.T
        zero = jnp.zeros_like(re_w)
        re_top = jnp.where(row < col, re_w, jnp.where(row > col, -re_t, zero))
        re_low = jnp.where(row > col, re_w, jnp.where(row < col, -re_t, zero))
        im_top = jnp.where(row <= col, im_w, im_t)
        im_low = jnp.where(row > col, im_w, jnp.where(row < col, im_t, re_w))
        for t, top, low in ((0, re_top, re_low), (1, im_top, im_low)):
            at = (2 * n + t) * modes
            m_ref[:half, at : at + half] = top.astype(BF16)
            m_ref[:half, at + half : at + modes] = src_ref[base + 2 * t + 1]
            m_ref[half:, at : at + half] = zero.astype(BF16)
            m_ref[half:, at + half : at + modes] = low.astype(BF16)
    slot = slot_ref[...]
    mode = lax.broadcasted_iota(jnp.int32, (slots, modes), 1)
    i = mode // TM
    start = i * tiles - (i * (i - 1)) // 2
    in_row = (slot >= start) & (slot < start + tiles - i)
    i_of = jnp.max(jnp.where(in_row, i, 0), axis=1, keepdims=True)
    j_of = slot - (i_of * tiles - (i_of * (i_of - 1)) // 2) + i_of
    in_col = jnp.concatenate([(i == j_of).astype(F32)] * (2 * count), axis=1)
    wide = -(-entries // LANES) * LANES
    place_row = lax.broadcasted_iota(jnp.int32, (2 * count * modes, wide), 0)
    place_col = lax.broadcasted_iota(jnp.int32, (2 * count * modes, wide), 1)
    target = (place_row // modes) * (TM * TM) + place_row % TM
    place = (target == place_col).astype(F32).astype(BF16)
    total = jnp.zeros((slots, wide), F32)
    for r in range(TM):
        pick = (mode == i_of * TM + r).astype(F32).astype(BF16)
        rows = jnp.dot(pick, m_ref[...], preferred_element_type=F32)
        found = jnp.dot((rows * in_col).astype(BF16), place, preferred_element_type=F32)
        total = total + (found if r == 0 else pltpu.roll(found, TM * r, 1))
    out_ref[...] = total[:, :entries] * scale


def per_device(eigvecs, link_seed, ownership):
    modes, _, _, layers, sites = eigvecs.shape
    size = lax.axis_size("sx")
    me = lax.axis_index("sx")
    half = modes // 2
    part = modes // PARTS
    extent_x = layers * size
    v = [
        eigvecs[j * part : (j + 1) * part].transpose(1, 2, 3, 0, 4).reshape(6, part, sites)
        for j in range(PARTS)
    ]
    near = [from_behind(block, "sx", -1) for block in v]
    slots = ownership.shape[0] // size
    own = lax.dynamic_slice_in_dim(ownership, me * slots, slots).reshape(slots, 1)
    scale = 1.0 / math.sqrt(12.0 * extent_x * sites)
    vmem = pl.BlockSpec(memory_space=pltpu.VMEM)
    link_shape = (1, 18, sites // LANES, LANES)
    plane = (6, modes, sites)
    negated = pltpu.VMEM((3, modes, sites), BF16)
    large = pltpu.CompilerParams(vmem_limit_bytes=LARGE)
    small = pltpu.CompilerParams(vmem_limit_bytes=SMALL)

    w_yz, u_x = pl.pallas_call(
        yz_kernel,
        out_shape=(
            jax.ShapeDtypeStruct((8, half, half), F32),
            jax.ShapeDtypeStruct(link_shape, F32),
        ),
        in_specs=[pl.BlockSpec(memory_space=pltpu.SMEM)] + [vmem] * PARTS,
        out_specs=(vmem, vmem),
        scratch_shapes=[
            pltpu.VMEM((2,) + link_shape[1:], F32),
            pltpu.VMEM(plane, BF16),
            pltpu.VMEM(plane, BF16),
            negated,
        ],
        compiler_params=large,
        name="products_yz",
    )(link_seed, *v)
    part_yz = sum_over_cores(w_yz)
    done = []
    for j in range(PARTS):
        last = j == PARTS - 1
        shape = (4, half, half) if last else (2 * modes, part)
        operands = [u_x, *v, near[j]] + (done if last else [])
        done.append(
            pl.pallas_call(
                functools.partial(x_kernel, PARTS),
                out_shape=jax.ShapeDtypeStruct(shape, F32),
                in_specs=[vmem] * len(operands),
                out_specs=vmem,
                scratch_shapes=[pltpu.VMEM((6, part, sites), BF16), negated],
                compiler_params=large,
                name="products_x" + str(j),
            )(*operands)
        )
    sum_x, sum_yz = sum_over_sites(done[-1], part_yz)
    return pl.pallas_call(
        functools.partial(tiles_kernel, scale),
        out_shape=jax.ShapeDtypeStruct((slots, 6 * TM * TM), F32),
        in_specs=[vmem] * 3,
        out_specs=vmem,
        scratch_shapes=[pltpu.VMEM((modes, 6 * modes), BF16)],
        compiler_params=small,
        name="own_tiles",
    )(own, sum_x, sum_yz)


def solution(mesh):
    return jax.shard_map(
        per_device,
        mesh=mesh,
        in_specs=(P("cfg", None, None, "sx", None), P("cfg"), P()),
        out_specs=P(("cfg", "sx"), None),
        check_vma=False,
    )
```

```python
import functools
import math

import jax
import jax.numpy as jnp
from jax import lax
from jax.experimental import pallas as pl
from jax.experimental.pallas import tpu as pltpu
from jax.sharding import PartitionSpec as P

TM = 4
NZ = 64
MODULUS = 46337
LANES = 128
ROWS = 16
PARTS = 2
LARGE = 32 * 1024 * 1024
SMALL = 8 * 1024 * 1024
MESH = pl.DeviceIdType.MESH
F32 = jnp.float32
BF16 = jnp.bfloat16


def from_behind(block, axis, distance):
    devices = range(lax.axis_size(axis))
    route = [((i - distance) % len(devices), i) for i in devices]
    return lax.ppermute(block, axis, route)


def quotient(value):
    q = jnp.floor(value.astype(F32) * (1.0 / MODULUS)).astype(jnp.int32)
    rest = value - q * MODULUS
    q = jnp.where(rest < 0, q - 1, jnp.where(rest >= MODULUS, q + 1, q))
    return q


def modulo(value):
    return value - quotient(value) * MODULUS


def links(seed, first_site, shape):
    code = (
        first_site
        + lax.broadcasted_iota(jnp.int32, shape, 0) * LANES
        + lax.broadcasted_iota(jnp.int32, shape, 1)
    )
    high = quotient(code)
    low = code - high * MODULUS
    mixed = modulo(seed * seed + low)
    mixed = modulo(mixed * mixed + high * 977 + 31)
    th = []
    for k in range(7):
        g = modulo(mixed + (5171 * k + 1))
        g = modulo(g * g + low)
        g = modulo(g * g + 12345)
        th.append(g.astype(F32) * (2.0 * math.pi / MODULUS) - math.pi)
    ca, sa = jnp.cos(th[0]), jnp.sin(th[0])
    cb, sb = jnp.cos(th[1]), jnp.sin(th[1])
    cg, sg = jnp.cos(th[2]), jnp.sin(th[2])
    rot = [
        [ca * cb * cg - sa * sg, -ca * cb * sg - sa * cg, ca * sb],
        [sa * cb * cg + ca * sg, -sa * cb * sg + ca * cg, sa * sb],
        [-sb * cg, sb * sg, cb],
    ]
    left = [th[3], th[4], -th[3] - th[4]]
    right = [th[5], th[6], -th[5] - th[6]]
    real, imag = [], []
    for r in range(3):
        for c in range(3):
            angle = left[r] + right[c]
            real.append(rot[r][c] * jnp.cos(angle))
            imag.append(rot[r][c] * jnp.sin(angle))
    return real + imag


def shift_plane(v_refs, sv_ref, kind):
    wide = 2 * LANES
    part, sites = v_refs[0].shape[1], v_refs[0].shape[2]
    row = lax.broadcasted_iota(jnp.int32, (wide, wide), 0)
    col = lax.broadcasted_iota(jnp.int32, (wide, wide), 1)
    if kind == 1:
        source = col + NZ
    else:
        source = jnp.where(col % NZ == NZ - 1, col - (NZ - 1), col + 1)
    move = (row == source).astype(F32).astype(BF16)
    carry_in = (row + wide == source).astype(F32).astype(BF16)[:LANES]
    for j, v_ref in enumerate(v_refs):
        rows = slice(j * part, (j + 1) * part)

        def component(q, carry, v_ref=v_ref, rows=rows):
            for at in range(0, sites, wide):
                x = jnp.dot(v_ref[q, :, at : at + wide], move, preferred_element_type=F32)
                if kind == 1:
                    after = (at + wide) % sites
                    x = x + jnp.dot(
                        v_ref[q, :, after : after + LANES],
                        carry_in,
                        preferred_element_type=F32,
                    )
                sv_ref[q, rows, at : at + wide] = x.astype(BF16)
            return carry

        lax.fori_loop(0, 6, component, 0)


def fill_hops(u_ref, d, src_ref, h_ref):
    modes, sites = src_ref.shape[1], src_ref.shape[2]

    def chunk_step(k, carry):
        u = [
            jnp.broadcast_to(u_ref[d, e, pl.ds(k, 1), :], (8, LANES)) for e in range(18)
        ]
        at = pl.ds(pl.multiple_of(k * LANES, LANES), LANES)

        def rows_step(g, carry):
            rows = pl.ds(pl.multiple_of(g * ROWS, ROWS), ROWS)
            vec = [src_ref[q, rows, at].astype(F32) for q in range(6)]
            parts = []
            for lo in (0, 8):
                v = [x[lo : lo + 8] for x in vec]
                out = []
                for c in range(3):
                    re = im = None
                    for s in range(3):
                        ur, ui = u[3 * c + s], u[9 + 3 * c + s]
                        a = ur * v[s] - ui * v[3 + s]
                        b = ur * v[3 + s] + ui * v[s]
                        re = a if re is None else re + a
                        im = b if im is None else im + b
                    out.append((re, im))
                parts.append(out)
            for c in range(3):
                for t in range(2):
                    both = jnp.concatenate([parts[0][c][t], parts[1][c][t]], 0)
                    h_ref[3 * t + c, rows, at] = both.astype(BF16)
            return carry

        return lax.fori_loop(0, modes // ROWS, rows_step, carry, unroll=2)

    lax.fori_loop(0, sites // LANES, chunk_step, 0)


def negate_imag(v_refs, nv_ref):
    part = v_refs[0].shape[1]
    for j, v_ref in enumerate(v_refs):
        for c in range(3):
            nv_ref[c, j * part : (j + 1) * part] = -v_ref[3 + c]


def gram(v_refs, nv_ref, h_ref):
    total = None
    for q in range(6):
        if q < 3:
            tail = [nv_ref[q]]
        else:
            tail = [r[q - 3] for r in v_refs]
        left = jnp.concatenate([r[q] for r in v_refs] + tail, 0)
        term = lax.dot_general(
            left, h_ref[q], (((1,), (1,)), ((), ())), preferred_element_type=F32
        )
        total = term if total is None else total + term
    return total


def pack_products(total, w_ref, base):
    modes = total.shape[0] // 2
    half = modes // 2
    re, im = total[:modes], total[modes:]
    row = lax.broadcasted_iota(jnp.int32, (half, half), 0)
    col = lax.broadcasted_iota(jnp.int32, (half, half), 1)
    re_top = re[:half, :half] - re[:half, :half].T
    re_low = re[half:, half:] - re[half:, half:].T
    im_top = im[:half, :half] + im[:half, :half].T
    im_low = im[half:, half:] + im[half:, half:].T
    re_mix = jnp.where(row < col, re_top, re_low)
    w_ref[base] = jnp.where(row == col, im_low, re_mix)
    w_ref[base + 1] = re[:half, half:] - re[half:, :half].T
    w_ref[base + 2] = jnp.where(row <= col, im_top, im_low)
    w_ref[base + 3] = im[:half, half:] + im[half:, :half].T


def yz_kernel(seed_ref, *refs):
    v_refs, (w_ref, ux_ref, u_ref, sv_ref, h_ref, nv_ref) = refs[:-6], refs[-6:]
    sites = v_refs[0].shape[2]
    shape = (sites // LANES, LANES)
    first = lax.axis_index("sx") * sites
    for d in (1, 2, 0):
        for e, entry in enumerate(links(seed_ref[d], first, shape)):
            if d == 0:
                ux_ref[0, e] = entry
            else:
                u_ref[d - 1, e] = entry
    negate_imag(v_refs, nv_ref)
    for d in (0, 1):
        shift_plane(v_refs, sv_ref, d + 1)
        fill_hops(u_ref, d, sv_ref, h_ref)
        pack_products(gram(v_refs, nv_ref, h_ref), w_ref, 4 * d)


def x_kernel(parts, ux_ref, *refs):
    v_refs, near_ref, rest = refs[:parts], refs[parts], refs[parts + 1 :]
    done_refs, (out_ref, h_ref, nv_ref) = rest[:-3], rest[-3:]
    negate_imag(v_refs, nv_ref)
    fill_hops(ux_ref, 0, near_ref, h_ref)
    total = gram(v_refs, nv_ref, h_ref)
    if len(done_refs) == 0 and out_ref.ndim == 2:
        out_ref[...] = total
    else:
        pack_products(
            jnp.concatenate([r[...] for r in done_refs] + [total], 1), out_ref, 0
        )


def copy_to(src, dst, sems, row, step, device):
    return pltpu.make_async_remote_copy(
        src_ref=src,
        dst_ref=dst,
        send_sem=sems.at[row, step],
        recv_sem=sems.at[row + 1, step],
        device_id=device,
        device_id_type=MESH,
    )


def core_sum_kernel(w_ref, out_ref, got, sems):
    me = lax.axis_index("sx")
    core = lax.rem(me, 2)
    partner = (lax.axis_index("cfg"), (me // 2) * 2 + 1 - core)
    barrier = pltpu.get_barrier_semaphore()
    pl.semaphore_signal(barrier, inc=1, device_id=partner, device_id_type=MESH)
    pl.semaphore_wait(barrier, 1)
    copy = copy_to(w_ref.at[1 - core], got, sems, 0, 0, partner)
    copy.start()
    copy.wait()
    out_ref[...] = (w_ref[core] + got[...]).astype(BF16)


def sum_kernel(chips, w_ref, yz_ref, x_out, yz_out, got, send, came, mine, full, sems):
    me = lax.axis_index("sx")
    cfg = lax.axis_index("cfg")
    core = lax.rem(me, 2)
    chip = me // 2
    other = 1 - core
    partner = (cfg, chip * 2 + other)
    rows = w_ref.shape[2]

    def chip_at(step):
        return lax.rem(chip + step, chips)

    def same_core(step):
        return (cfg, chip_at(step) * 2 + core)

    barrier = pltpu.get_barrier_semaphore()
    pl.semaphore_signal(barrier, inc=1, device_id=partner, device_id_type=MESH)
    for step in range(1, chips):
        pl.semaphore_signal(
            barrier, inc=1, device_id=same_core(step), device_id_type=MESH
        )
    pl.semaphore_wait(barrier, chips)

    order = list(range(1, chips)) + [0]
    halves, pieces, back = {}, {}, {}
    for step in order:
        to = chip_at(step)
        halves[step] = copy_to(w_ref.at[other, to], got.at[to], sems, 0, step, partner)
        halves[step].start()
    for step in order[:-1]:
        to = chip_at(step)
        send[to, rows:] = yz_ref[to]
        halves[step].wait_recv()
        send[to, :rows] = (w_ref[core, to] + got[to]).astype(BF16)
        pieces[step] = copy_to(
            send.at[to], came.at[step], sems, 2, step, same_core(step)
        )
        pieces[step].start()
    halves[0].wait_recv()
    total = jnp.concatenate(
        [w_ref[core, chip] + got[chip], yz_ref[chip].astype(F32)], 0
    )
    for step in order[:-1]:
        pieces[step].wait_recv()
        total = total + came[step].astype(F32)
    mine[...] = total.astype(BF16)
    full[core, chip] = total.astype(BF16)

    for step in order[:-1]:
        back[step] = copy_to(mine, full.at[core, chip], sems, 4, step, same_core(step))
        back[step].start()
    passed = [copy_to(mine, full.at[core, chip], sems, 6, 0, partner)]
    passed[0].start()
    for step in order[:-1]:
        origin = lax.rem(chip + chips - step, chips)
        block = full.at[core, origin]
        back[step].wait_recv()
        passed.append(copy_to(block, block, sems, 6, step, partner))
        passed[-1].start()
    for copy in passed:
        copy.wait()
    for step in order:
        halves[step].wait_send()
    for step in order[:-1]:
        pieces[step].wait_send()
        back[step].wait_send()
    x_out[...] = full[:, :, :rows]
    yz_out[...] = full[:, :, rows:]


def split_rows(w):
    size = lax.axis_size("sx")
    blocks, rows, lanes = w.shape
    return w.reshape(2, size // 2, blocks * rows // size, lanes)


def sum_over_cores(w):
    parts = split_rows(w)
    vmem = pl.BlockSpec(memory_space=pltpu.VMEM)
    return pl.pallas_call(
        core_sum_kernel,
        out_shape=jax.ShapeDtypeStruct(parts.shape[1:], BF16),
        in_specs=[vmem],
        out_specs=vmem,
        scratch_shapes=[
            pltpu.VMEM(parts.shape[1:], F32),
            pltpu.SemaphoreType.DMA((2, 1)),
        ],
        compiler_params=pltpu.CompilerParams(
            collective_id=0, has_side_effects=True, vmem_limit_bytes=SMALL
        ),
        name="sum_over_cores",
    )(parts)


def sum_over_sites(w, part_yz):
    parts = split_rows(w)
    _, chips, rows, lanes = parts.shape
    rows_yz = part_yz.shape[1]
    both = (chips, rows + rows_yz, lanes)
    vmem = pl.BlockSpec(memory_space=pltpu.VMEM)
    x, yz = pl.pallas_call(
        functools.partial(sum_kernel, chips),
        out_shape=(
            jax.ShapeDtypeStruct((2, chips, rows, lanes), BF16),
            jax.ShapeDtypeStruct((2, chips, rows_yz, lanes), BF16),
        ),
        in_specs=[vmem] * 2,
        out_specs=(vmem, vmem),
        scratch_shapes=[
            pltpu.VMEM((chips, rows, lanes), F32),
            pltpu.VMEM(both, BF16),
            pltpu.VMEM(both, BF16),
            pltpu.VMEM(both[1:], BF16),
            pltpu.VMEM((2,) + both, BF16),
            pltpu.SemaphoreType.DMA((8, chips)),
        ],
        compiler_params=pltpu.CompilerParams(
            collective_id=1, has_side_effects=True, vmem_limit_bytes=SMALL
        ),
        name="sum_over_sites",
    )(parts, part_yz)
    return x.reshape(w.shape), yz.reshape(-1, *w.shape[1:])


def tiles_kernel(scale, slot_ref, x_ref, yz_ref, out_ref, m_ref):
    half = x_ref.shape[1]
    modes = 2 * half
    tiles = modes // TM
    count = 3
    slots, entries = out_ref.shape
    row = lax.broadcasted_iota(jnp.int32, (half, half), 0)
    col = lax.broadcasted_iota(jnp.int32, (half, half), 1)
    for n in range(count):
        src_ref, base = (x_ref, 0) if n == 0 else (yz_ref, 4 * n - 4)
        re_w = src_ref[base].astype(F32)
        im_w = src_ref[base + 2].astype(F32)
        re_t, im_t = re_w.T, im_w.T
        zero = jnp.zeros_like(re_w)
        re_top = jnp.where(row < col, re_w, jnp.where(row > col, -re_t, zero))
        re_low = jnp.where(row > col, re_w, jnp.where(row < col, -re_t, zero))
        im_top = jnp.where(row <= col, im_w, im_t)
        im_low = jnp.where(row > col, im_w, jnp.where(row < col, im_t, re_w))
        for t, top, low in ((0, re_top, re_low), (1, im_top, im_low)):
            at = (2 * n + t) * modes
            m_ref[:half, at : at + half] = top.astype(BF16)
            m_ref[:half, at + half : at + modes] = src_ref[base + 2 * t + 1]
            m_ref[half:, at : at + half] = zero.astype(BF16)
            m_ref[half:, at + half : at + modes] = low.astype(BF16)
    slot = slot_ref[...]
    mode = lax.broadcasted_iota(jnp.int32, (slots, modes), 1)
    i = mode // TM
    start = i * tiles - (i * (i - 1)) // 2
    in_row = (slot >= start) & (slot < start + tiles - i)
    i_of = jnp.max(jnp.where(in_row, i, 0), axis=1, keepdims=True)
    j_of = slot - (i_of * tiles - (i_of * (i_of - 1)) // 2) + i_of
    in_col = jnp.concatenate([(i == j_of).astype(F32)] * (2 * count), axis=1)
    wide = -(-entries // LANES) * LANES
    place_row = lax.broadcasted_iota(jnp.int32, (2 * count * modes, wide), 0)
    place_col = lax.broadcasted_iota(jnp.int32, (2 * count * modes, wide), 1)
    target = (place_row // modes) * (TM * TM) + place_row % TM
    place = (target == place_col).astype(F32).astype(BF16)
    total = jnp.zeros((slots, wide), F32)
    for r in range(TM):
        pick = (mode == i_of * TM + r).astype(F32).astype(BF16)
        rows = jnp.dot(pick, m_ref[...], preferred_element_type=F32)
        found = jnp.dot((rows * in_col).astype(BF16), place, preferred_element_type=F32)
        total = total + (found if r == 0 else pltpu.roll(found, TM * r, 1))
    out_ref[...] = total[:, :entries] * scale


def per_device(eigvecs, link_seed, ownership):
    modes, _, _, layers, sites = eigvecs.shape
    size = lax.axis_size("sx")
    me = lax.axis_index("sx")
    half = modes // 2
    part = modes // PARTS
    extent_x = layers * size
    v = [
        eigvecs[j * part : (j + 1) * part].transpose(1, 2, 3, 0, 4).reshape(6, part, sites)
        for j in range(PARTS)
    ]
    near = [from_behind(block, "sx", -1) for block in v]
    slots = ownership.shape[0] // size
    own = lax.dynamic_slice_in_dim(ownership, me * slots, slots).reshape(slots, 1)
    scale = 1.0 / math.sqrt(12.0 * extent_x * sites)
    vmem = pl.BlockSpec(memory_space=pltpu.VMEM)
    link_shape = (1, 18, sites // LANES, LANES)
    plane = (6, modes, sites)
    negated = pltpu.VMEM((3, modes, sites), BF16)
    large = pltpu.CompilerParams(vmem_limit_bytes=LARGE)
    small = pltpu.CompilerParams(vmem_limit_bytes=SMALL)

    w_yz, u_x = pl.pallas_call(
        yz_kernel,
        out_shape=(
            jax.ShapeDtypeStruct((8, half, half), F32),
            jax.ShapeDtypeStruct(link_shape, F32),
        ),
        in_specs=[pl.BlockSpec(memory_space=pltpu.SMEM)] + [vmem] * PARTS,
        out_specs=(vmem, vmem),
        scratch_shapes=[
            pltpu.VMEM((2,) + link_shape[1:], F32),
            pltpu.VMEM(plane, BF16),
            pltpu.VMEM(plane, BF16),
            negated,
        ],
        compiler_params=large,
        name="products_yz",
    )(link_seed, *v)
    part_yz = sum_over_cores(w_yz)
    done = []
    for j in range(PARTS):
        last = j == PARTS - 1
        shape = (4, half, half) if last else (2 * modes, part)
        operands = [u_x, *v, near[j]] + (done if last else [])
        done.append(
            pl.pallas_call(
                functools.partial(x_kernel, PARTS),
                out_shape=jax.ShapeDtypeStruct(shape, F32),
                in_specs=[vmem] * len(operands),
                out_specs=vmem,
                scratch_shapes=[pltpu.VMEM((6, part, sites), BF16), negated],
                compiler_params=large,
                name="products_x" + str(j),
            )(*operands)
        )
    sum_x, sum_yz = sum_over_sites(done[-1], part_yz)
    return pl.pallas_call(
        functools.partial(tiles_kernel, scale),
        out_shape=jax.ShapeDtypeStruct((slots, 6 * TM * TM), F32),
        in_specs=[vmem] * 3,
        out_specs=vmem,
        scratch_shapes=[pltpu.VMEM((modes, 6 * modes), BF16)],
        compiler_params=small,
        name="own_tiles",
    )(own, sum_x, sum_yz)


def solution(mesh):
    return jax.shard_map(
        per_device,
        mesh=mesh,
        in_specs=(P("cfg", None, None, "sx", None), P("cfg"), P()),
        out_specs=P(("cfg", "sx"), None),
        check_vma=False,
    )
```
